32 devices in a mesh: grp: 2 (over x), tmpl: 8 (over z, y), tm: 2 (over core).
Axes of the slice: x: 2, y: 2, z: 4, core: 2. Of those that a mesh axis runs over, the one named last changes fastest.
Arguments:
- spectra: bfloat16 [1024, 4, 8192], P(('grp', 'tm', 'tmpl')), parts along dimension 0, may hold values from -6 to 6
- offsets: int32 [1024, 16], P(('grp', 'tm'), 'tmpl'), parts along dimension 0, may hold values from 0 to 1008
- fractions: float32 [4096], P(('grp', 'tmpl')), parts along dimension 0, may hold values from 0.1 to 0.9
- antenna: float32 [1024, 4], P('grp'), parts along dimension 0, may hold values from -2 to 2, as said below
- starts: int32 [64], P('grp'), parts along dimension 0, may hold values from 0 to 255
- durations: int32 [64], P('grp'), parts along dimension 0, may hold values from 48 to 256
Outputs:
- fstat_map: float32 [32, 32, 4096], P('tm', None, ('grp', 'tmpl')), parts along dimension 2
- loudest: float32 [64, 32], P(('grp', 'tm')), parts along dimension 0
The draws below stay inside these ranges and needn't reach their ends.
There are 2 independent parts, one for each index of `grp`. The reference program is written for one: setup_inputs(seed, part) draws one part's arguments, and reference() takes and returns one part's arrays. A program takes and returns all parts, laid end to end along the dimension named above; each array names one. Nothing has to cross between parts.
Inputs may be any that keep to these rules, and one draw needn't show every extreme that they name: `antenna`: each detector's responses a and b turn once every 48 SFTs with magnitudes that vary from SFT to SFT.
All inputs are finite; a program needn't handle non-finite values.
Results may differ from the reference program's by a relative error of at most 0.0051.
Values may be sent and summed in bfloat16 or wider, within the bound.
A program may use at most 128 MiB of HBM per device.

```python
import jax
import jax.numpy as jnp
from jax import lax

W = 16
TPB = 128
NG = 32
DAY = 48
BAND_DEV = 1024
NB_DEV = 2
NSFT = 512
NBLK = 16
QTOT = 2048
BINS = 8192


def draw_antenna(key, part):
    key_phase, key_size, key_jitter = jax.random.split(key, 3)
    sft_axis = jnp.arange(NSFT, dtype=jnp.float32)[:, None]
    start_phase = jax.random.uniform(key_phase, (1, 2), jnp.float32, 0.0, 2.0 * jnp.pi)
    magnitude = jax.random.uniform(key_size, (NSFT, 2), jnp.float32, 0.5, 1.5)
    jitter = jax.random.uniform(key_jitter, (NSFT, 2), jnp.float32, -0.6, 0.6)
    turn_angle = 2.0 * jnp.pi * sft_axis / DAY + start_phase + jitter
    return jnp.concatenate([magnitude * jnp.cos(turn_angle), magnitude * jnp.sin(turn_angle)], axis=1)


def plant(values, own_key, smallest, top_value):
    index_at = [jax.random.randint(jax.random.fold_in(own_key, axis), (), 0, length) for axis, length in enumerate(values.shape)]
    main_axis = values.shape.index(max(values.shape))
    next_to = index_at[:main_axis] + [(index_at[main_axis] + 1) % values.shape[main_axis]] + index_at[main_axis + 1:]
    return values.at[tuple(index_at)].set(smallest).at[tuple(next_to)].set(top_value)


def shard_levels(rng, extent, cuts, smallest, high):
    def one(position, blocks):
        heights = jax.random.uniform(jax.random.fold_in(jax.random.fold_in(rng, 6), position), (blocks,), jnp.float32, smallest / len(cuts), high / len(cuts))
        return jnp.repeat(jnp.exp(heights), extent[position] // blocks).reshape((-1,) + (1,) * (len(extent) - position - 1))

    level = one(*cuts[0])
    for cut in cuts[1:]:
        level = level * one(*cut)
    return level


def noise(rng, dims, width, limit, cuts=(), held_as=jnp.bfloat16):
    drawn = width * jax.random.normal(rng, dims, jnp.float32)
    if cuts:
        drawn = drawn * shard_levels(rng, dims, cuts, -0.22, 0.18)
    return jnp.clip(drawn, -limit, limit).astype(held_as)


def setup_inputs(seed: int = 0, part: int = 0) -> dict:
    key_of = jax.random.split(jax.random.key(seed), 7)
    own_keys = jax.random.split(jax.random.fold_in(key_of[6], part), 7)
    spectra = noise(own_keys[0], (NSFT, 4, BINS), 1.0, 6.0, ((0, 16),))
    offsets = plant(jax.random.randint(own_keys[1], (NSFT, NBLK), 0, BAND_DEV - W + 1), jax.random.fold_in(own_keys[1], 1), 0, BAND_DEV - W).astype(jnp.int32)
    fractions = jnp.clip(0.1 + 0.79999997 * jax.random.uniform(own_keys[2], (QTOT,), jnp.float32) ** shard_levels(own_keys[2], (QTOT,), ((0, 8),), -0.2, 0.2), 0.1, 0.9)
    antenna = draw_antenna(jax.random.fold_in(jax.random.fold_in(key_of[6], part), 71), part)
    starts = plant(jax.random.randint(own_keys[4], (NG,), 0, NSFT // 2), jax.random.fold_in(own_keys[4], 1), 0, (NSFT // 2) - 1).astype(jnp.int32)
    durations = plant(jax.random.randint(own_keys[5], (NG,), DAY, NSFT // 2 + 1), jax.random.fold_in(own_keys[5], 1), DAY, (NSFT // 2 + 1) - 1).astype(jnp.int32)
    return dict(spectra=spectra, offsets=offsets, fractions=fractions, antenna=antenna, starts=starts, durations=durations)


def pick_bins(spectrum, places):
    return spectrum[:, places]


def weigh(windows, antenna):
    values = windows.astype(jnp.float32)
    detector_one = values[:, 0:2]
    detector_two = values[:, 2:4]
    weighted_a = antenna[:, 0][:, None, None, None] * detector_one + antenna[:, 1][:, None, None, None] * detector_two
    weighted_b = antenna[:, 2][:, None, None, None] * detector_one + antenna[:, 3][:, None, None, None] * detector_two
    return jnp.concatenate([weighted_a, weighted_b], axis=1).astype(jnp.bfloat16)


def dirichlet(fractions):
    bin_shift = jnp.arange(W, dtype=jnp.float32)
    distance = fractions[:, None] + (W // 2 - 1) - bin_shift[None, :]
    parity = (jnp.arange(W, dtype=jnp.int32) % 2).astype(jnp.float32)
    alternate = 1.0 - 2.0 * parity
    return (alternate[None, :] * jnp.sin(jnp.pi * fractions)[:, None] / (jnp.pi * distance)).astype(jnp.bfloat16)


def antenna_prefix(antenna):
    along_a = antenna[:, 0] * antenna[:, 0] + antenna[:, 1] * antenna[:, 1]
    along_b = antenna[:, 2] * antenna[:, 2] + antenna[:, 3] * antenna[:, 3]
    across = antenna[:, 0] * antenna[:, 2] + antenna[:, 1] * antenna[:, 3]
    stacked = jnp.stack([along_a, along_b, across], axis=1)
    return jnp.concatenate([jnp.zeros((1, 3), jnp.float32), jnp.cumsum(stacked, axis=0)], axis=0)


def statistic(interval, weights):
    real_a = interval[..., 0, :]
    imag_a = interval[..., 1, :]
    real_b = interval[..., 2, :]
    imag_b = interval[..., 3, :]
    weight_a = weights[..., 0:1]
    weight_b = weights[..., 1:2]
    weight_c = weights[..., 2:3]
    numerator = weight_b * (real_a * real_a + imag_a * imag_a) + weight_a * (real_b * real_b + imag_b * imag_b) - 2.0 * weight_c * (real_a * real_b + imag_a * imag_b)
    return numerator / (weight_a * weight_b - weight_c * weight_c)


def reference(spectra, offsets, fractions, antenna, starts, durations):
    band_start = (jnp.arange(NBLK, dtype=jnp.int32) // NB_DEV) * BAND_DEV
    bin_index = offsets[:, :, None] + band_start[None, :, None] + jnp.arange(W, dtype=jnp.int32)[None, None, :]
    windows = jax.vmap(pick_bins)(spectra, bin_index)
    weighted = weigh(windows, antenna)
    kernel = dirichlet(fractions).reshape(NBLK, TPB, W)
    atom_rows = jnp.einsum("scbm,bqm->scbq", weighted.astype(jnp.float32), kernel.astype(jnp.float32), precision=lax.Precision.HIGHEST)
    atom_rows = atom_rows.reshape(NSFT, 4 * QTOT)
    running = jnp.concatenate([jnp.zeros((1, 4 * QTOT), jnp.float32), jnp.cumsum(atom_rows, axis=0)], axis=0)
    end_points = starts[None, :] + durations[:, None]
    interval = running[end_points] - running[starts][None]
    cum_weights = antenna_prefix(antenna)
    weights = cum_weights[end_points] - cum_weights[starts][None]
    fstat_map = statistic(interval.reshape(NG, NG, 4, QTOT), weights)
    loudest = jnp.max(fstat_map, axis=2)
    return fstat_map, loudest
```

```python
import functools

import jax
import jax.numpy as jnp
from jax import lax
from jax.experimental import pallas as pl
from jax.experimental.pallas import tpu as pltpu
from jax.sharding import PartitionSpec as P

W = 16
LANES = 128
F32 = jnp.float32
BF16 = jnp.bfloat16
MESH = pl.DeviceIdType.MESH


def split3(x):
    hi = x.astype(BF16)
    rest = x - hi.astype(F32)
    mid = rest.astype(BF16)
    return hi, mid, (rest - mid.astype(F32)).astype(BF16)


def fused(
    cfg,
    off_ref, spec_ref, frac_ref, ant_ref, starts_ref, dur_ref,
    fstat_ref, loud_ref,
    xbuf, xf, off_send, off_recv, wsend, wall, mask, lsend, lrecv,
    spec_sem, osend_sem, orecv_sem, wsend_sem, wrecv_sem, lsend_sem, lrecv_sem,
):
    bands, times, rows, nb, chunks, nsft, grid, my_rows = cfg
    t_me = lax.axis_index("tmpl")
    m_me = lax.axis_index("tm")
    group = bands * times
    me = m_me * bands + t_me

    spec_copy = pltpu.make_async_copy(spec_ref, xbuf, spec_sem)
    spec_copy.start()

    barrier = pltpu.get_barrier_semaphore()

    def greet(k, carry):
        peer = lax.rem(me + k, group)
        pl.semaphore_signal(
            barrier, inc=1,
            device_id={"tmpl": lax.rem(peer, bands), "tm": lax.div(peer, bands)},
            device_id_type=MESH,
        )
        return carry

    lax.fori_loop(1, group, greet, 0)

    off_send[...] = jnp.zeros_like(off_send)
    for t in range(bands):
        off_send[t, 0:nb, 0:rows] = off_ref[:, t * rows:(t + 1) * rows]
    off_recv[t_me] = off_send[t_me]
    pl.semaphore_wait(barrier, group - 1)

    def off_copy(k):
        peer = lax.rem(t_me + k, bands)
        return pltpu.make_async_remote_copy(
            src_ref=off_send.at[peer], dst_ref=off_recv.at[t_me],
            send_sem=osend_sem.at[peer], recv_sem=orecv_sem.at[t_me],
            device_id={"tmpl": peer}, device_id_type=MESH,
        )

    def off_arrival(k):
        source = lax.rem(t_me + k, bands)
        return pltpu.make_async_remote_copy(
            src_ref=off_send.at[source], dst_ref=off_recv.at[source],
            send_sem=osend_sem.at[source], recv_sem=orecv_sem.at[source],
            device_id={"tmpl": source}, device_id_type=MESH,
        )

    def start_off(k, carry):
        off_copy(k).start()
        return carry

    lax.fori_loop(1, bands, start_off, 0)

    spec_copy.wait()

    def widen(i, carry):
        pair = jnp.concatenate(
            [xbuf[2 * i].astype(F32), xbuf[2 * i + 1].astype(F32)], axis=0
        )
        at = pl.ds(pl.multiple_of(i * 8, 8), 8)
        for ch in range(bands * chunks):
            xf[ch, at, :] = pair[:, ch * LANES:(ch + 1) * LANES]
        return carry

    lax.fori_loop(0, rows // 2, widen, 0)

    lane = lax.broadcasted_iota(jnp.int32, (rows, LANES), 1)
    lane_m = lane % W
    lane_b = (lane // W) % nb
    lane_c = lane // (W * nb)
    ant_t = jnp.transpose(
        jnp.concatenate([ant_ref[...], jnp.zeros((4, nsft), F32)], axis=0)
    )
    mine = jnp.zeros((rows, 8), F32)
    for slot in range(group):
        mine = jnp.where(slot == me, ant_t[slot * rows:(slot + 1) * rows, :], mine)
    upper = lane_c < 2
    coef_p = jnp.where(upper, mine[:, 0:1], mine[:, 2:3])
    coef_q = jnp.where(upper, mine[:, 1:2], mine[:, 3:4])
    even = (lane_c % 2) == 0

    def window_copy(t, m):
        return pltpu.make_async_remote_copy(
            src_ref=wsend.at[t], dst_ref=wall.at[me],
            send_sem=wsend_sem.at[m * bands + t], recv_sem=wrecv_sem.at[me],
            device_id={"tmpl": t, "tm": m}, device_id_type=MESH,
        )

    def pick(k, carry):
        t = lax.rem(t_me + k, bands)

        @pl.when(k < bands)
        def _():
            off_arrival(k).wait_recv()

        columns = jnp.transpose(off_recv[t])[0:rows, :]
        place = jnp.zeros((rows, LANES), jnp.int32)
        for b in range(nb):
            place = jnp.where(lane_b == b, columns[:, b:b + 1], place)
        place = place + lane_m
        chunk = place // LANES
        spot = place % LANES
        picked = [jnp.zeros((rows, LANES), F32) for _ in range(4)]
        for ch in range(chunks):
            here = chunk == ch
            for c in range(4):
                piece = xf[t * chunks + ch, pl.ds(c, rows, stride=4), :]
                got = jnp.take_along_axis(piece, spot, axis=1, mode="promise_in_bounds")
                picked[c] = jnp.where(here, got, picked[c])
        one = jnp.where(even, picked[0], picked[1])
        two = jnp.where(even, picked[2], picked[3])
        wsend[t] = (coef_p * one + coef_q * two).astype(BF16)
        for m in range(times):
            @pl.when(jnp.logical_or(t != t_me, m != m_me))
            def _():
                window_copy(t, m).start()
        return carry

    lax.fori_loop(1, bands + 1, pick, 0)
    wall[me] = wsend[t_me]

    row = lax.broadcasted_iota(jnp.int32, (grid, LANES), 0)
    begin = jnp.zeros((grid, LANES), jnp.int32)
    for i in range(grid):
        begin = jnp.where(row == i, starts_ref[i], begin)
    begin = jnp.concatenate([begin] * (nsft // LANES), axis=1)
    sft = lax.broadcasted_iota(jnp.int32, (grid, nsft), 1)
    since = sft - begin
    for j in range(my_rows):
        length = dur_ref[m_me * my_rows + j]
        inside = jnp.logical_and(since >= 0, since < length)
        mask[j * grid:(j + 1) * grid, :] = inside.astype(F32).astype(BF16)

    ant = ant_ref[...]
    a1, a2, b1, b2 = ant[0:1], ant[1:2], ant[2:3], ant[3:4]
    terms = jnp.concatenate(
        [a1 * a1 + a2 * a2, b1 * b1 + b2 * b2, a1 * b1 + a2 * b2, jnp.zeros((5, nsft), F32)],
        axis=0,
    )
    nt = (((1,), (1,)), ((), ()))
    sums = 0.0
    for piece in split3(terms):
        sums = sums + lax.dot_general(mask[...], piece, nt, preferred_element_type=F32)

    width = frac_ref.shape[1]
    fracs = frac_ref[...]
    shift = lax.broadcasted_iota(jnp.int32, (W, width), 0)
    alternate = (1 - 2 * (shift % 2)).astype(F32)
    distance = fracs + (W // 2 - 1) - shift.astype(F32)
    dirichlet = alternate * jnp.sin(jnp.pi * fracs) / (jnp.pi * distance)
    tiled = jnp.concatenate([dirichlet] * (4 * nb), axis=0)
    feature = lax.broadcasted_iota(jnp.int32, tiled.shape, 0)
    block = lax.broadcasted_iota(jnp.int32, tiled.shape, 1) // (width // nb)
    same = (feature // W) % nb == block
    bases = []
    for c in range(4):
        base = jnp.where(jnp.logical_and(same, feature // (W * nb) == c), tiled, 0.0)
        base = base.astype(BF16)
        bases.append(jnp.concatenate([base, base], axis=0))

    def window_arrival(k):
        source = lax.rem(me + k, group)
        return pltpu.make_async_remote_copy(
            src_ref=wsend.at[0], dst_ref=wall.at[source],
            send_sem=wsend_sem.at[source], recv_sem=wrecv_sem.at[source],
            device_id={"tmpl": lax.rem(source, bands), "tm": lax.div(source, bands)},
            device_id_type=MESH,
        )

    def arrive(k, carry):
        window_arrival(k).wait_recv()
        return carry

    lax.fori_loop(1, group, arrive, 0)
    everything = wall[...].reshape(nsft, LANES)

    step = 128
    for r in range(my_rows * grid // step):
        at = slice(r * step, (r + 1) * step)
        total = jnp.dot(mask[at, :], everything, preferred_element_type=F32)
        hi = total.astype(BF16)
        lo = (total - hi.astype(F32)).astype(BF16)
        both = jnp.concatenate([hi, lo], axis=1)
        ra, ia, rb, ib = [jnp.dot(both, base, preferred_element_type=F32) for base in bases]
        wa, wb, wc = sums[at, 0:1], sums[at, 1:2], sums[at, 2:3]
        inverse = 1.0 / (wa * wb - wc * wc)
        top = wb * (ra * ra + ia * ia) + wa * (rb * rb + ib * ib) - (2.0 * wc) * (ra * rb + ia * ib)
        stat = top * inverse
        fstat_ref[at, :] = stat
        best = stat[:, 0:LANES]
        for q in range(1, width // LANES):
            best = jnp.maximum(best, stat[:, q * LANES:(q + 1) * LANES])
        lsend[0:1, at] = jnp.max(jnp.transpose(best), axis=0, keepdims=True)

    def loud_copy(k):
        peer = lax.rem(t_me + k, bands)
        return pltpu.make_async_remote_copy(
            src_ref=lsend, dst_ref=lrecv.at[t_me],
            send_sem=lsend_sem.at[peer], recv_sem=lrecv_sem.at[t_me],
            device_id={"tmpl": peer}, device_id_type=MESH,
        )

    def loud_arrival(k):
        source = lax.rem(t_me + k, bands)
        return pltpu.make_async_remote_copy(
            src_ref=lsend, dst_ref=lrecv.at[source],
            send_sem=lsend_sem.at[source], recv_sem=lrecv_sem.at[source],
            device_id={"tmpl": source}, device_id_type=MESH,
        )

    def start_loud(k, carry):
        loud_copy(k).start()
        return carry

    lax.fori_loop(1, bands, start_loud, 0)

    def window_done(k, carry):
        peer = lax.rem(me + k, group)
        window_copy(lax.rem(peer, bands), lax.div(peer, bands)).wait_send()
        return carry

    lax.fori_loop(1, group, window_done, 0)

    def off_done(k, carry):
        off_copy(k).wait_send()
        return carry

    lax.fori_loop(1, bands, off_done, 0)
    lrecv[t_me] = lsend[...]

    def loud_arrive(k, carry):
        loud_arrival(k).wait_recv()
        return carry

    lax.fori_loop(1, bands, loud_arrive, 0)
    most = lrecv[0]
    for t in range(1, bands):
        most = jnp.maximum(most, lrecv[t])
    for j in range(my_rows):
        loud_ref[j:j + 1, :] = most[:, j * grid:(j + 1) * grid]

    def loud_done(k, carry):
        loud_copy(k).wait_send()
        return carry

    lax.fori_loop(1, bands, loud_done, 0)


def body(spectra, offsets, fractions, antenna, starts, durations):
    bands = lax.axis_size("tmpl")
    times = lax.axis_size("tm")
    rows, _, bins = spectra.shape
    nb = offsets.shape[1]
    width = fractions.shape[0]
    nsft = antenna.shape[0]
    grid = starts.shape[0]
    my_rows = grid // times
    chunks = bins // bands // LANES
    group = bands * times
    cells = my_rows * grid
    cfg = (bands, times, rows, nb, chunks, nsft, grid, my_rows)
    vmem = pl.BlockSpec(memory_space=pltpu.VMEM)
    smem = pl.BlockSpec(memory_space=pltpu.SMEM)
    fstat, loudest = pl.pallas_call(
        functools.partial(fused, cfg),
        out_shape=(
            jax.ShapeDtypeStruct((cells, width), F32),
            jax.ShapeDtypeStruct((my_rows, grid), F32),
        ),
        in_specs=[vmem, pl.BlockSpec(memory_space=pl.ANY), vmem, vmem, smem, smem],
        out_specs=(vmem, vmem),
        scratch_shapes=[
            pltpu.VMEM((rows, 4, bins), BF16),
            pltpu.VMEM((bins // LANES, rows * 4, LANES), F32),
            pltpu.VMEM((bands, 8, LANES), jnp.int32),
            pltpu.VMEM((bands, 8, LANES), jnp.int32),
            pltpu.VMEM((bands, rows, LANES), BF16),
            pltpu.VMEM((group, rows, LANES), BF16),
            pltpu.VMEM((cells, nsft), BF16),
            pltpu.VMEM((1, cells), F32),
            pltpu.VMEM((bands, 1, cells), F32),
            pltpu.SemaphoreType.DMA,
            pltpu.SemaphoreType.DMA((bands,)),
            pltpu.SemaphoreType.DMA((bands,)),
            pltpu.SemaphoreType.DMA((group,)),
            pltpu.SemaphoreType.DMA((group,)),
            pltpu.SemaphoreType.DMA((bands,)),
            pltpu.SemaphoreType.DMA((bands,)),
        ],
        compiler_params=pltpu.CompilerParams(
            collective_id=0, has_side_effects=True, vmem_limit_bytes=40 * 1024 * 1024
        ),
        name="transient_fstat",
    )(offsets.T, spectra, fractions.reshape(1, width), antenna.T, starts, durations)
    return fstat.reshape(my_rows, grid, width), loudest


def solution(mesh):
    in_specs = (
        P(("grp", "tm", "tmpl"), None, None),
        P(("grp", "tm"), "tmpl"),
        P(("grp", "tmpl")),
        P("grp", None),
        P("grp"),
        P("grp"),
    )
    out_specs = (P("tm", None, ("grp", "tmpl")), P(("grp", "tm"), None))
    return jax.shard_map(body, mesh=mesh, in_specs=in_specs, out_specs=out_specs, check_vma=False)
```

```python
import functools

import jax
import jax.numpy as jnp
from jax import lax
from jax.experimental import pallas as pl
from jax.experimental.pallas import tpu as pltpu
from jax.sharding import PartitionSpec as P

W = 16
LANES = 128
F32 = jnp.float32
BF16 = jnp.bfloat16
MESH = pl.DeviceIdType.MESH


def split3(x):
    hi = x.astype(BF16)
    rest = x - hi.astype(F32)
    mid = rest.astype(BF16)
    return hi, mid, (rest - mid.astype(F32)).astype(BF16)


def fused(
    cfg,
    off_in, spec_ref, frac_in, ant_in, starts_in, dur_in,
    fstat_out, loud_ref,
    off_ref, frac_ref, ant_ref, starts_ref, dur_ref, fstat_ref, small_sem, fstat_sem,
    xbuf, xf, off_send, off_recv, wsend, wall, mask, lsend, lrecv,
    spec_sem, osend_sem, orecv_sem, wsend_sem, wrecv_sem, lsend_sem, lrecv_sem,
):
    bands, times, rows, nb, chunks, nsft, grid, my_rows = cfg
    t_me = lax.axis_index("tmpl")
    m_me = lax.axis_index("tm")
    group = bands * times
    me = m_me * bands + t_me

    spec_copy = pltpu.make_async_copy(spec_ref, xbuf, spec_sem)
    small = [
        pltpu.make_async_copy(source, target, small_sem.at[n])
        for n, (source, target) in enumerate(
            [(off_in, off_ref), (starts_in, starts_ref), (dur_in, dur_ref), (ant_in, ant_ref), (frac_in, frac_ref)]
        )
    ]
    for copy in small:
        copy.start()
    spec_copy.start()

    barrier = pltpu.get_barrier_semaphore()

    def greet(k, carry):
        peer = lax.rem(me + k, group)
        pl.semaphore_signal(
            barrier, inc=1,
            device_id={"tmpl": lax.rem(peer, bands), "tm": lax.div(peer, bands)},
            device_id_type=MESH,
        )
        return carry

    lax.fori_loop(1, group, greet, 0)

    small[0].wait()
    off_send[...] = jnp.zeros_like(off_send)
    for t in range(bands):
        off_send[t, 0:nb, 0:rows] = off_ref[:, t * rows:(t + 1) * rows]
    off_recv[t_me] = off_send[t_me]
    small[1].wait()
    small[2].wait()
    row = lax.broadcasted_iota(jnp.int32, (grid, LANES), 0)
    begin = jnp.zeros((grid, LANES), jnp.int32)
    for i in range(grid):
        begin = jnp.where(row == i, starts_ref[i], begin)
    begin = jnp.concatenate([begin] * (nsft // LANES), axis=1)
    sft = lax.broadcasted_iota(jnp.int32, (grid, nsft), 1)
    since = sft - begin
    for j in range(my_rows):
        length = dur_ref[m_me * my_rows + j]
        inside = jnp.logical_and(since >= 0, since < length)
        mask[j * grid:(j + 1) * grid, :] = inside.astype(F32).astype(BF16)
    small[3].wait()
    small[4].wait()
    pl.semaphore_wait(barrier, group - 1)

    def off_copy(k):
        peer = lax.rem(t_me + k, bands)
        return pltpu.make_async_remote_copy(
            src_ref=off_send.at[peer], dst_ref=off_recv.at[t_me],
            send_sem=osend_sem.at[peer], recv_sem=orecv_sem.at[t_me],
            device_id={"tmpl": peer}, device_id_type=MESH,
        )

    def off_arrival(k):
        source = lax.rem(t_me + k, bands)
        return pltpu.make_async_remote_copy(
            src_ref=off_send.at[source], dst_ref=off_recv.at[source],
            send_sem=osend_sem.at[source], recv_sem=orecv_sem.at[source],
            device_id={"tmpl": source}, device_id_type=MESH,
        )

    def start_off(k, carry):
        off_copy(k).start()
        return carry

    lax.fori_loop(1, bands, start_off, 0)

    spec_copy.wait()

    def widen(i, carry):
        pair = jnp.concatenate(
            [xbuf[2 * i].astype(F32), xbuf[2 * i + 1].astype(F32)], axis=0
        )
        at = pl.ds(pl.multiple_of(i * 8, 8), 8)
        for ch in range(bands * chunks):
            xf[ch, at, :] = pair[:, ch * LANES:(ch + 1) * LANES]
        return carry

    lax.fori_loop(0, rows // 2, widen, 0)

    lane = lax.broadcasted_iota(jnp.int32, (rows, LANES), 1)
    lane_m = lane % W
    lane_b = (lane // W) % nb
    lane_c = lane // (W * nb)
    ant_t = jnp.transpose(
        jnp.concatenate([ant_ref[...], jnp.zeros((4, nsft), F32)], axis=0)
    )
    mine = jnp.zeros((rows, 8), F32)
    for slot in range(group):
        mine = jnp.where(slot == me, ant_t[slot * rows:(slot + 1) * rows, :], mine)
    upper = lane_c < 2
    coef_p = jnp.where(upper, mine[:, 0:1], mine[:, 2:3])
    coef_q = jnp.where(upper, mine[:, 1:2], mine[:, 3:4])
    even = (lane_c % 2) == 0

    def window_copy(t, m):
        return pltpu.make_async_remote_copy(
            src_ref=wsend.at[t], dst_ref=wall.at[me],
            send_sem=wsend_sem.at[m * bands + t], recv_sem=wrecv_sem.at[me],
            device_id={"tmpl": t, "tm": m}, device_id_type=MESH,
        )

    def pick(k, carry):
        t = lax.rem(t_me + k, bands)

        @pl.when(k < bands)
        def _():
            off_arrival(k).wait_recv()

        columns = jnp.transpose(off_recv[t])[0:rows, :]
        place = jnp.zeros((rows, LANES), jnp.int32)
        for b in range(nb):
            place = jnp.where(lane_b == b, columns[:, b:b + 1], place)
        place = place + lane_m
        chunk = place // LANES
        spot = place % LANES
        picked = [jnp.zeros((rows, LANES), F32) for _ in range(4)]
        for ch in range(chunks):
            here = chunk == ch
            for c in range(4):
                piece = xf[t * chunks + ch, pl.ds(c, rows, stride=4), :]
                got = jnp.take_along_axis(piece, spot, axis=1, mode="promise_in_bounds")
                picked[c] = jnp.where(here, got, picked[c])
        one = jnp.where(even, picked[0], picked[1])
        two = jnp.where(even, picked[2], picked[3])
        wsend[t] = (coef_p * one + coef_q * two).astype(BF16)
        for m in range(times):
            @pl.when(jnp.logical_or(t != t_me, m != m_me))
            def _():
                window_copy(t, m).start()
        return carry

    lax.fori_loop(1, bands + 1, pick, 0)
    wall[me] = wsend[t_me]

    ant = ant_ref[...]
    a1, a2, b1, b2 = ant[0:1], ant[1:2], ant[2:3], ant[3:4]
    terms = jnp.concatenate(
        [a1 * a1 + a2 * a2, b1 * b1 + b2 * b2, a1 * b1 + a2 * b2, jnp.zeros((5, nsft), F32)],
        axis=0,
    )
    nt = (((1,), (1,)), ((), ()))
    sums = 0.0
    for piece in split3(terms):
        sums = sums + lax.dot_general(mask[...], piece, nt, preferred_element_type=F32)

    width = frac_ref.shape[1]
    fracs = frac_ref[...]
    shift = lax.broadcasted_iota(jnp.int32, (W, width), 0)
    alternate = (1 - 2 * (shift % 2)).astype(F32)
    distance = fracs + (W // 2 - 1) - shift.astype(F32)
    dirichlet = alternate * jnp.sin(jnp.pi * fracs) / (jnp.pi * distance)
    tiled = jnp.concatenate([dirichlet] * (4 * nb), axis=0)
    feature = lax.broadcasted_iota(jnp.int32, tiled.shape, 0)
    block = lax.broadcasted_iota(jnp.int32, tiled.shape, 1) // (width // nb)
    same = (feature // W) % nb == block
    bases = []
    for c in range(4):
        base = jnp.where(jnp.logical_and(same, feature // (W * nb) == c), tiled, 0.0)
        base = base.astype(BF16)
        bases.append(jnp.concatenate([base, base], axis=0))

    def window_arrival(k):
        source = lax.rem(me + k, group)
        return pltpu.make_async_remote_copy(
            src_ref=wsend.at[0], dst_ref=wall.at[source],
            send_sem=wsend_sem.at[source], recv_sem=wrecv_sem.at[source],
            device_id={"tmpl": lax.rem(source, bands), "tm": lax.div(source, bands)},
            device_id_type=MESH,
        )

    def arrive(k, carry):
        window_arrival(k).wait_recv()
        return carry

    lax.fori_loop(1, group, arrive, 0)
    everything = wall[...].reshape(nsft, LANES)

    step = 128

    def fstat_copy(r):
        part = pl.ds(r * step, step)
        return pltpu.make_async_copy(fstat_ref.at[part], fstat_out.at[part], fstat_sem.at[r])

    for r in range(my_rows * grid // step):
        at = slice(r * step, (r + 1) * step)
        total = jnp.dot(mask[at, :], everything, preferred_element_type=F32)
        hi = total.astype(BF16)
        lo = (total - hi.astype(F32)).astype(BF16)
        both = jnp.concatenate([hi, lo], axis=1)
        ra, ia, rb, ib = [jnp.dot(both, base, preferred_element_type=F32) for base in bases]
        wa, wb, wc = sums[at, 0:1], sums[at, 1:2], sums[at, 2:3]
        inverse = 1.0 / (wa * wb - wc * wc)
        top = wb * (ra * ra + ia * ia) + wa * (rb * rb + ib * ib) - (2.0 * wc) * (ra * rb + ia * ib)
        stat = top * inverse
        fstat_ref[at, :] = stat
        fstat_copy(r).start()
        best = stat[:, 0:LANES]
        for q in range(1, width // LANES):
            best = jnp.maximum(best, stat[:, q * LANES:(q + 1) * LANES])
        lsend[0:1, at] = jnp.max(jnp.transpose(best), axis=0, keepdims=True)

    def loud_copy(k):
        peer = lax.rem(t_me + k, bands)
        return pltpu.make_async_remote_copy(
            src_ref=lsend, dst_ref=lrecv.at[t_me],
            send_sem=lsend_sem.at[peer], recv_sem=lrecv_sem.at[t_me],
            device_id={"tmpl": peer}, device_id_type=MESH,
        )

    def loud_arrival(k):
        source = lax.rem(t_me + k, bands)
        return pltpu.make_async_remote_copy(
            src_ref=lsend, dst_ref=lrecv.at[source],
            send_sem=lsend_sem.at[source], recv_sem=lrecv_sem.at[source],
            device_id={"tmpl": source}, device_id_type=MESH,
        )

    def start_loud(k, carry):
        loud_copy(k).start()
        return carry

    lax.fori_loop(1, bands, start_loud, 0)

    def window_done(k, carry):
        peer = lax.rem(me + k, group)
        window_copy(lax.rem(peer, bands), lax.div(peer, bands)).wait_send()
        return carry

    lax.fori_loop(1, group, window_done, 0)

    def off_done(k, carry):
        off_copy(k).wait_send()
        return carry

    lax.fori_loop(1, bands, off_done, 0)
    lrecv[t_me] = lsend[...]

    def loud_arrive(k, carry):
        loud_arrival(k).wait_recv()
        return carry

    lax.fori_loop(1, bands, loud_arrive, 0)
    most = lrecv[0]
    for t in range(1, bands):
        most = jnp.maximum(most, lrecv[t])
    for j in range(my_rows):
        loud_ref[j:j + 1, :] = most[:, j * grid:(j + 1) * grid]

    def loud_done(k, carry):
        loud_copy(k).wait_send()
        return carry

    lax.fori_loop(1, bands, loud_done, 0)
    for r in range(my_rows * grid // step):
        fstat_copy(r).wait()


def body(spectra, offsets, fractions, antenna, starts, durations):
    bands = lax.axis_size("tmpl")
    times = lax.axis_size("tm")
    rows, _, bins = spectra.shape
    nb = offsets.shape[1]
    width = fractions.shape[0]
    nsft = antenna.shape[0]
    grid = starts.shape[0]
    my_rows = grid // times
    chunks = bins // bands // LANES
    group = bands * times
    cells = my_rows * grid
    cfg = (bands, times, rows, nb, chunks, nsft, grid, my_rows)
    vmem = pl.BlockSpec(memory_space=pltpu.VMEM)
    anywhere = pl.BlockSpec(memory_space=pl.ANY)
    fstat, loudest = pl.pallas_call(
        functools.partial(fused, cfg),
        out_shape=(
            jax.ShapeDtypeStruct((cells, width), F32),
            jax.ShapeDtypeStruct((my_rows, grid), F32),
        ),
        in_specs=[anywhere] * 6,
        out_specs=(anywhere, vmem),
        scratch_shapes=[
            pltpu.VMEM((nb, offsets.shape[0]), jnp.int32),
            pltpu.VMEM((1, width), F32),
            pltpu.VMEM((4, nsft), F32),
            pltpu.SMEM((grid,), jnp.int32),
            pltpu.SMEM((grid,), jnp.int32),
            pltpu.VMEM((cells, width), F32),
            pltpu.SemaphoreType.DMA((5,)),
            pltpu.SemaphoreType.DMA((cells // 128,)),
            pltpu.VMEM((rows, 4, bins), BF16),
            pltpu.VMEM((bins // LANES, rows * 4, LANES), F32),
            pltpu.VMEM((bands, 8, LANES), jnp.int32),
            pltpu.VMEM((bands, 8, LANES), jnp.int32),
            pltpu.VMEM((bands, rows, LANES), BF16),
            pltpu.VMEM((group, rows, LANES), BF16),
            pltpu.VMEM((cells, nsft), BF16),
            pltpu.VMEM((1, cells), F32),
            pltpu.VMEM((bands, 1, cells), F32),
            pltpu.SemaphoreType.DMA,
            pltpu.SemaphoreType.DMA((bands,)),
            pltpu.SemaphoreType.DMA((bands,)),
            pltpu.SemaphoreType.DMA((group,)),
            pltpu.SemaphoreType.DMA((group,)),
            pltpu.SemaphoreType.DMA((bands,)),
            pltpu.SemaphoreType.DMA((bands,)),
        ],
        compiler_params=pltpu.CompilerParams(
            collective_id=0, has_side_effects=True, vmem_limit_bytes=60 * 1024 * 1024
        ),
        name="transient_fstat",
    )(offsets.T, spectra, fractions.reshape(1, width), antenna.T, starts, durations)
    return fstat.reshape(my_rows, grid, width), loudest


def solution(mesh):
    in_specs = (
        P(("grp", "tm", "tmpl"), None, None),
        P(("grp", "tm"), "tmpl"),
        P(("grp", "tmpl")),
        P("grp", None),
        P("grp"),
        P("grp"),
    )
    out_specs = (P("tm", None, ("grp", "tmpl")), P(("grp", "tm"), None))
    return jax.shard_map(body, mesh=mesh, in_specs=in_specs, out_specs=out_specs, check_vma=False)
```

```python
import functools

import jax
import jax.numpy as jnp
from jax import lax
from jax.experimental import pallas as pl
from jax.experimental.pallas import tpu as pltpu
from jax.sharding import PartitionSpec as P

W = 16
LANES = 128
F32 = jnp.float32
BF16 = jnp.bfloat16
MESH = pl.DeviceIdType.MESH


def split3(x):
    hi = x.astype(BF16)
    rest = x - hi.astype(F32)
    mid = rest.astype(BF16)
    return hi, mid, (rest - mid.astype(F32)).astype(BF16)


def fused(
    cfg,
    off_in, spec_ref, frac_in, ant_in, starts_in, dur_in,
    fstat_ref, loud_ref,
    off_ref, frac_ref, ant_ref, starts_ref, dur_ref, small_sem,
    xbuf, xf, off_send, off_recv, places, wsend, wall, mask, lsend, lrecv,
    spec_sem, osend_sem, orecv_sem, wsend_sem, wrecv_sem, lsend_sem, lrecv_sem,
):
    bands, times, rows, nb, chunks, nsft, grid, my_rows = cfg
    t_me = lax.axis_index("tmpl")
    m_me = lax.axis_index("tm")
    group = bands * times
    me = m_me * bands + t_me

    spec_copy = pltpu.make_async_copy(spec_ref, xbuf, spec_sem)
    small = [
        pltpu.make_async_copy(source, target, small_sem.at[n])
        for n, (source, target) in enumerate(
            [(off_in, off_ref), (starts_in, starts_ref), (dur_in, dur_ref), (ant_in, ant_ref), (frac_in, frac_ref)]
        )
    ]
    for copy in small:
        copy.start()
    spec_copy.start()

    barrier = pltpu.get_barrier_semaphore()

    def greet(k, carry):
        peer = lax.rem(me + k, group)
        pl.semaphore_signal(
            barrier, inc=1,
            device_id={"tmpl": lax.rem(peer, bands), "tm": lax.div(peer, bands)},
            device_id_type=MESH,
        )
        return carry

    lax.fori_loop(1, group, greet, 0)

    small[0].wait()
    off_send[...] = jnp.zeros_like(off_send)
    for t in range(bands):
        off_send[t, :, 0:rows] = off_ref[:, t * rows:(t + 1) * rows]
    off_recv[t_me] = off_send[t_me]
    small[1].wait()
    small[2].wait()
    row = lax.broadcasted_iota(jnp.int32, (grid, LANES), 0)
    begin = jnp.zeros((grid, LANES), jnp.int32)
    for i in range(grid):
        begin = jnp.where(row == i, starts_ref[i], begin)
    begin = jnp.concatenate([begin] * (nsft // LANES), axis=1)
    sft = lax.broadcasted_iota(jnp.int32, (grid, nsft), 1)
    since = sft - begin
    for j in range(my_rows):
        length = dur_ref[m_me * my_rows + j]
        inside = jnp.logical_and(since >= 0, since < length)
        mask[j * grid:(j + 1) * grid, :] = inside.astype(F32).astype(BF16)
    small[3].wait()
    small[4].wait()
    pl.semaphore_wait(barrier, group - 1)

    def off_copy(k):
        peer = lax.rem(t_me + k, bands)
        return pltpu.make_async_remote_copy(
            src_ref=off_send.at[peer], dst_ref=off_recv.at[t_me],
            send_sem=osend_sem.at[peer], recv_sem=orecv_sem.at[t_me],
            device_id={"tmpl": peer}, device_id_type=MESH,
        )

    def off_arrival(k):
        source = lax.rem(t_me + k, bands)
        return pltpu.make_async_remote_copy(
            src_ref=off_send.at[source], dst_ref=off_recv.at[source],
            send_sem=osend_sem.at[source], recv_sem=orecv_sem.at[source],
            device_id={"tmpl": source}, device_id_type=MESH,
        )

    def start_off(k, carry):
        off_copy(k).start()
        return carry

    lax.fori_loop(1, bands, start_off, 0)

    spec_copy.wait()

    def widen(i, carry):
        pair = jnp.concatenate(
            [xbuf[2 * i].astype(F32), xbuf[2 * i + 1].astype(F32)], axis=0
        )
        at = pl.ds(pl.multiple_of(i * 8, 8), 8)
        for ch in range(bands * chunks):
            xf[ch, at, :] = pair[:, ch * LANES:(ch + 1) * LANES]
        return carry

    lax.fori_loop(0, rows // 2, widen, 0)

    lane = lax.broadcasted_iota(jnp.int32, (rows, LANES), 1)
    lane_m = lane % W
    lane_b = (lane // W) % nb
    lane_c = lane // (W * nb)
    ant_t = jnp.transpose(
        jnp.concatenate([ant_ref[...], jnp.zeros((4, nsft), F32)], axis=0)
    )
    mine = jnp.zeros((rows, 8), F32)
    for slot in range(group):
        mine = jnp.where(slot == me, ant_t[slot * rows:(slot + 1) * rows, :], mine)
    upper = lane_c < 2
    coef_p = jnp.where(upper, mine[:, 0:1], mine[:, 2:3])
    coef_q = jnp.where(upper, mine[:, 1:2], mine[:, 3:4])
    even = (lane_c % 2) == 0

    def window_copy(t, m):
        return pltpu.make_async_remote_copy(
            src_ref=wsend.at[t], dst_ref=wall.at[me],
            send_sem=wsend_sem.at[m * bands + t], recv_sem=wrecv_sem.at[me],
            device_id={"tmpl": t, "tm": m}, device_id_type=MESH,
        )

    def off_arrive(k, carry):
        off_arrival(k).wait_recv()
        return carry

    lax.fori_loop(1, bands, off_arrive, 0)
    columns = jnp.transpose(
        jnp.concatenate([off_recv[t] for t in range(bands)], axis=0)
    )[0:rows, :]
    for t in range(bands):
        place = jnp.zeros((rows, LANES), jnp.int32)
        for b in range(nb):
            at = t * nb + b
            place = jnp.where(lane_b == b, columns[:, at:at + 1], place)
        places[t] = place + lane_m

    def pick(k, carry):
        t = lax.rem(t_me + k, bands)

        place = places[t]
        chunk = place // LANES
        spot = place % LANES
        picked = [jnp.zeros((rows, LANES), F32) for _ in range(4)]
        for ch in range(chunks):
            here = chunk == ch
            for c in range(4):
                piece = xf[t * chunks + ch, pl.ds(c, rows, stride=4), :]
                got = jnp.take_along_axis(piece, spot, axis=1, mode="promise_in_bounds")
                picked[c] = jnp.where(here, got, picked[c])
        one = jnp.where(even, picked[0], picked[1])
        two = jnp.where(even, picked[2], picked[3])
        wsend[t] = (coef_p * one + coef_q * two).astype(BF16)
        for m in range(times):
            @pl.when(jnp.logical_or(t != t_me, m != m_me))
            def _():
                window_copy(t, m).start()
        return carry

    lax.fori_loop(1, bands + 1, pick, 0)
    wall[me] = wsend[t_me]

    ant = ant_ref[...]
    a1, a2, b1, b2 = ant[0:1], ant[1:2], ant[2:3], ant[3:4]
    terms = jnp.concatenate(
        [a1 * a1 + a2 * a2, b1 * b1 + b2 * b2, a1 * b1 + a2 * b2, jnp.zeros((5, nsft), F32)],
        axis=0,
    )
    nt = (((1,), (1,)), ((), ()))
    sums = 0.0
    for piece in split3(terms):
        sums = sums + lax.dot_general(mask[...], piece, nt, preferred_element_type=F32)

    width = frac_ref.shape[1]
    fracs = frac_ref[...]
    shift = lax.broadcasted_iota(jnp.int32, (W, width), 0)
    alternate = (1 - 2 * (shift % 2)).astype(F32)
    distance = fracs + (W // 2 - 1) - shift.astype(F32)
    dirichlet = alternate * jnp.sin(jnp.pi * fracs) / (jnp.pi * distance)
    tiled = jnp.concatenate([dirichlet] * (4 * nb), axis=0)
    feature = lax.broadcasted_iota(jnp.int32, tiled.shape, 0)
    block = lax.broadcasted_iota(jnp.int32, tiled.shape, 1) // (width // nb)
    same = (feature // W) % nb == block
    bases = []
    for c in range(4):
        base = jnp.where(jnp.logical_and(same, feature // (W * nb) == c), tiled, 0.0)
        base = base.astype(BF16)
        bases.append(jnp.concatenate([base, base], axis=0))

    def window_arrival(k):
        source = lax.rem(me + k, group)
        return pltpu.make_async_remote_copy(
            src_ref=wsend.at[0], dst_ref=wall.at[source],
            send_sem=wsend_sem.at[source], recv_sem=wrecv_sem.at[source],
            device_id={"tmpl": lax.rem(source, bands), "tm": lax.div(source, bands)},
            device_id_type=MESH,
        )

    def arrive(k, carry):
        window_arrival(k).wait_recv()
        return carry

    lax.fori_loop(1, group, arrive, 0)
    everything = wall[...].reshape(nsft, LANES)

    step = 128

    for r in range(my_rows * grid // step):
        at = slice(r * step, (r + 1) * step)
        total = jnp.dot(mask[at, :], everything, preferred_element_type=F32)
        hi = total.astype(BF16)
        lo = (total - hi.astype(F32)).astype(BF16)
        both = jnp.concatenate([hi, lo], axis=1)
        ra, ia, rb, ib = [jnp.dot(both, base, preferred_element_type=F32) for base in bases]
        wa, wb, wc = sums[at, 0:1], sums[at, 1:2], sums[at, 2:3]
        inverse = 1.0 / (wa * wb - wc * wc)
        top = wb * (ra * ra + ia * ia) + wa * (rb * rb + ib * ib) - (2.0 * wc) * (ra * rb + ia * ib)
        stat = top * inverse
        fstat_ref[at, :] = stat
        best = stat[:, 0:LANES]
        for q in range(1, width // LANES):
            best = jnp.maximum(best, stat[:, q * LANES:(q + 1) * LANES])
        lsend[0:1, at] = jnp.max(jnp.transpose(best), axis=0, keepdims=True)

    def loud_copy(k):
        peer = lax.rem(t_me + k, bands)
        return pltpu.make_async_remote_copy(
            src_ref=lsend, dst_ref=lrecv.at[t_me],
            send_sem=lsend_sem.at[peer], recv_sem=lrecv_sem.at[t_me],
            device_id={"tmpl": peer}, device_id_type=MESH,
        )

    def loud_arrival(k):
        source = lax.rem(t_me + k, bands)
        return pltpu.make_async_remote_copy(
            src_ref=lsend, dst_ref=lrecv.at[source],
            send_sem=lsend_sem.at[source], recv_sem=lrecv_sem.at[source],
            device_id={"tmpl": source}, device_id_type=MESH,
        )

    def start_loud(k, carry):
        loud_copy(k).start()
        return carry

    lax.fori_loop(1, bands, start_loud, 0)

    def window_done(k, carry):
        peer = lax.rem(me + k, group)
        window_copy(lax.rem(peer, bands), lax.div(peer, bands)).wait_send()
        return carry

    lax.fori_loop(1, group, window_done, 0)

    def off_done(k, carry):
        off_copy(k).wait_send()
        return carry

    lax.fori_loop(1, bands, off_done, 0)
    lrecv[t_me] = lsend[...]

    def loud_arrive(k, carry):
        loud_arrival(k).wait_recv()
        return carry

    lax.fori_loop(1, bands, loud_arrive, 0)
    most = lrecv[0]
    for t in range(1, bands):
        most = jnp.maximum(most, lrecv[t])
    for j in range(my_rows):
        loud_ref[j:j + 1, :] = most[:, j * grid:(j + 1) * grid]

    def loud_done(k, carry):
        loud_copy(k).wait_send()
        return carry

    lax.fori_loop(1, bands, loud_done, 0)


def body(spectra, offsets, fractions, antenna, starts, durations):
    bands = lax.axis_size("tmpl")
    times = lax.axis_size("tm")
    rows, _, bins = spectra.shape
    nb = offsets.shape[1]
    width = fractions.shape[0]
    nsft = antenna.shape[0]
    grid = starts.shape[0]
    my_rows = grid // times
    chunks = bins // bands // LANES
    group = bands * times
    cells = my_rows * grid
    cfg = (bands, times, rows, nb, chunks, nsft, grid, my_rows)
    vmem = pl.BlockSpec(memory_space=pltpu.VMEM)
    anywhere = pl.BlockSpec(memory_space=pltpu.HBM)
    fstat, loudest = pl.pallas_call(
        functools.partial(fused, cfg),
        out_shape=(
            jax.ShapeDtypeStruct((cells, width), F32),
            jax.ShapeDtypeStruct((my_rows, grid), F32),
        ),
        in_specs=[anywhere] * 6,
        out_specs=(vmem, vmem),
        scratch_shapes=[
            pltpu.VMEM((nb, offsets.shape[0]), jnp.int32),
            pltpu.VMEM((1, width), F32),
            pltpu.VMEM((4, nsft), F32),
            pltpu.SMEM((grid,), jnp.int32),
            pltpu.SMEM((grid,), jnp.int32),
            pltpu.SemaphoreType.DMA((5,)),
            pltpu.VMEM((rows, 4, bins), BF16),
            pltpu.VMEM((bins // LANES, rows * 4, LANES), F32),
            pltpu.VMEM((bands, nb, LANES), jnp.int32),
            pltpu.VMEM((bands, nb, LANES), jnp.int32),
            pltpu.VMEM((bands, rows, LANES), jnp.int32),
            pltpu.VMEM((bands, rows, LANES), BF16),
            pltpu.VMEM((group, rows, LANES), BF16),
            pltpu.VMEM((cells, nsft), BF16),
            pltpu.VMEM((1, cells), F32),
            pltpu.VMEM((bands, 1, cells), F32),
            pltpu.SemaphoreType.DMA,
            pltpu.SemaphoreType.DMA((bands,)),
            pltpu.SemaphoreType.DMA((bands,)),
            pltpu.SemaphoreType.DMA((group,)),
            pltpu.SemaphoreType.DMA((group,)),
            pltpu.SemaphoreType.DMA((bands,)),
            pltpu.SemaphoreType.DMA((bands,)),
        ],
        compiler_params=pltpu.CompilerParams(
            collective_id=0, has_side_effects=True, vmem_limit_bytes=32 * 1024 * 1024
        ),
        name="transient_fstat",
    )(*[
        pltpu.with_memory_space_constraint(x, pltpu.HBM)
        for x in (offsets.T, spectra, fractions.reshape(1, width), antenna.T, starts, durations)
    ])
    return fstat.reshape(my_rows, grid, width), loudest


def solution(mesh):
    in_specs = (
        P(("grp", "tm", "tmpl"), None, None),
        P(("grp", "tm"), "tmpl"),
        P(("grp", "tmpl")),
        P("grp", None),
        P("grp"),
        P("grp"),
    )
    out_specs = (P("tm", None, ("grp", "tmpl")), P(("grp", "tm"), None))
    return jax.shard_map(body, mesh=mesh, in_specs=in_specs, out_specs=out_specs, check_vma=False)
```

```python
import functools

import jax
import jax.numpy as jnp
from jax import lax
from jax.experimental import pallas as pl
from jax.experimental.pallas import tpu as pltpu
from jax.sharding import PartitionSpec as P

W = 16
LANES = 128
F32 = jnp.float32
BF16 = jnp.bfloat16
MESH = pl.DeviceIdType.MESH


def split3(x):
    hi = x.astype(BF16)
    rest = x - hi.astype(F32)
    mid = rest.astype(BF16)
    return hi, mid, (rest - mid.astype(F32)).astype(BF16)


def fused(
    cfg,
    off_in, spec_ref, frac_in, ant_in, starts_in, dur_in,
    fstat_ref, loud_ref,
    off_ref, frac_ref, ant_ref, starts_ref, dur_ref, small_sem,
    xbuf, xf, off_send, off_recv, places, wsend, wall, mask, lsend, lrecv,
    spec_sem, osend_sem, orecv_sem, wsend_sem, wrecv_sem, lsend_sem, lrecv_sem,
):
    bands, times, rows, nb, chunks, nsft, grid, my_rows = cfg
    t_me = lax.axis_index("tmpl")
    m_me = lax.axis_index("tm")
    group = bands * times
    me = m_me * bands + t_me

    spec_copy = pltpu.make_async_copy(spec_ref, xbuf, spec_sem)
    small = [
        pltpu.make_async_copy(source, target, small_sem.at[n])
        for n, (source, target) in enumerate(
            [(off_in, off_ref), (starts_in, starts_ref), (dur_in, dur_ref), (ant_in, ant_ref), (frac_in, frac_ref)]
        )
    ]
    for copy in small:
        copy.start()
    spec_copy.start()

    barrier = pltpu.get_barrier_semaphore()

    def greet(k, carry):
        peer = lax.rem(me + k, group)
        pl.semaphore_signal(
            barrier, inc=1,
            device_id={"tmpl": lax.rem(peer, bands), "tm": lax.div(peer, bands)},
            device_id_type=MESH,
        )
        return carry

    lax.fori_loop(1, group, greet, 0)

    small[0].wait()
    off_send[...] = jnp.zeros_like(off_send)
    for t in range(bands):
        off_send[t, :, 0:rows] = off_ref[:, t * rows:(t + 1) * rows]
    off_recv[t_me] = off_send[t_me]
    small[1].wait()
    small[2].wait()
    row = lax.broadcasted_iota(jnp.int32, (grid, LANES), 0)
    begin = jnp.zeros((grid, LANES), jnp.int32)
    for i in range(grid):
        begin = jnp.where(row == i, starts_ref[i], begin)
    begin = jnp.concatenate([begin] * (nsft // LANES), axis=1)
    sft = lax.broadcasted_iota(jnp.int32, (grid, nsft), 1)
    since = sft - begin
    for j in range(my_rows):
        length = dur_ref[m_me * my_rows + j]
        inside = jnp.logical_and(since >= 0, since < length)
        mask[j * grid:(j + 1) * grid, :] = inside.astype(F32).astype(BF16)
    small[3].wait()
    small[4].wait()
    pl.semaphore_wait(barrier, group - 1)

    def off_copy(k):
        peer = lax.rem(t_me + k, bands)
        return pltpu.make_async_remote_copy(
            src_ref=off_send.at[peer], dst_ref=off_recv.at[t_me],
            send_sem=osend_sem.at[peer], recv_sem=orecv_sem.at[t_me],
            device_id={"tmpl": peer}, device_id_type=MESH,
        )

    def off_arrival(k):
        source = lax.rem(t_me + k, bands)
        return pltpu.make_async_remote_copy(
            src_ref=off_send.at[source], dst_ref=off_recv.at[source],
            send_sem=osend_sem.at[source], recv_sem=orecv_sem.at[source],
            device_id={"tmpl": source}, device_id_type=MESH,
        )

    def start_off(k, carry):
        off_copy(k).start()
        return carry

    lax.fori_loop(1, bands, start_off, 0)

    spec_copy.wait()

    def widen(i, carry):
        pair = jnp.concatenate(
            [xbuf[2 * i].astype(F32), xbuf[2 * i + 1].astype(F32)], axis=0
        )
        at = pl.ds(pl.multiple_of(i * 8, 8), 8)
        for ch in range(bands * chunks):
            xf[ch, at, :] = pair[:, ch * LANES:(ch + 1) * LANES]
        return carry

    lax.fori_loop(0, rows // 2, widen, 0)

    lane = lax.broadcasted_iota(jnp.int32, (rows, LANES), 1)
    lane_m = lane % W
    lane_b = (lane // W) % nb
    lane_c = lane // (W * nb)
    ant_t = jnp.transpose(
        jnp.concatenate([ant_ref[...], jnp.zeros((4, nsft), F32)], axis=0)
    )
    mine = jnp.zeros((rows, 8), F32)
    for slot in range(group):
        mine = jnp.where(slot == me, ant_t[slot * rows:(slot + 1) * rows, :], mine)
    upper = lane_c < 2
    coef_p = jnp.where(upper, mine[:, 0:1], mine[:, 2:3])
    coef_q = jnp.where(upper, mine[:, 1:2], mine[:, 3:4])
    even = (lane_c % 2) == 0

    def window_copy(t, m):
        return pltpu.make_async_remote_copy(
            src_ref=wsend.at[t], dst_ref=wall.at[me],
            send_sem=wsend_sem.at[m * bands + t], recv_sem=wrecv_sem.at[me],
            device_id={"tmpl": t, "tm": m}, device_id_type=MESH,
        )

    def off_arrive(k, carry):
        off_arrival(k).wait_recv()
        return carry

    lax.fori_loop(1, bands, off_arrive, 0)
    columns = jnp.transpose(
        jnp.concatenate([off_recv[t] for t in range(bands)], axis=0)
    )[0:rows, :]
    for t in range(bands):
        for b in range(nb):
            at = t * nb + b
            places[at] = jnp.broadcast_to(columns[:, at:at + 1], (rows, LANES))

    def pick(k, carry):
        t = lax.rem(t_me + k, bands)

        picked = [None] * 4
        for b in range(nb):
            begin_b = places[t * nb + b]
            wanted = begin_b // LANES + (lane < begin_b % LANES).astype(jnp.int32)
            spot = (begin_b + lane_m) % LANES
            source = [jnp.zeros((rows, LANES), F32) for _ in range(4)]
            for ch in range(chunks):
                here = wanted == ch
                for c in range(4):
                    piece = xf[t * chunks + ch, pl.ds(c, rows, stride=4), :]
                    source[c] = jnp.where(here, piece, source[c])
            for c in range(4):
                got = jnp.take_along_axis(source[c], spot, axis=1, mode="promise_in_bounds")
                picked[c] = got if b == 0 else jnp.where(lane_b == b, got, picked[c])
        one = jnp.where(even, picked[0], picked[1])
        two = jnp.where(even, picked[2], picked[3])
        wsend[t] = (coef_p * one + coef_q * two).astype(BF16)
        for m in range(times):
            @pl.when(jnp.logical_or(t != t_me, m != m_me))
            def _():
                window_copy(t, m).start()
        return carry

    lax.fori_loop(1, bands + 1, pick, 0)
    wall[me] = wsend[t_me]

    ant = ant_ref[...]
    a1, a2, b1, b2 = ant[0:1], ant[1:2], ant[2:3], ant[3:4]
    terms = jnp.concatenate(
        [a1 * a1 + a2 * a2, b1 * b1 + b2 * b2, a1 * b1 + a2 * b2, jnp.zeros((5, nsft), F32)],
        axis=0,
    )
    nt = (((1,), (1,)), ((), ()))
    sums = 0.0
    for piece in split3(terms):
        sums = sums + lax.dot_general(mask[...], piece, nt, preferred_element_type=F32)

    width = frac_ref.shape[1]
    fracs = frac_ref[...]
    shift = lax.broadcasted_iota(jnp.int32, (W, width), 0)
    alternate = (1 - 2 * (shift % 2)).astype(F32)
    distance = fracs + (W // 2 - 1) - shift.astype(F32)
    dirichlet = alternate * jnp.sin(jnp.pi * fracs) / (jnp.pi * distance)
    tiled = jnp.concatenate([dirichlet] * (4 * nb), axis=0)
    feature = lax.broadcasted_iota(jnp.int32, tiled.shape, 0)
    block = lax.broadcasted_iota(jnp.int32, tiled.shape, 1) // (width // nb)
    same = (feature // W) % nb == block
    bases = []
    for c in range(4):
        base = jnp.where(jnp.logical_and(same, feature // (W * nb) == c), tiled, 0.0)
        base = base.astype(BF16)
        bases.append(jnp.concatenate([base, base], axis=0))

    def window_arrival(k):
        source = lax.rem(me + k, group)
        return pltpu.make_async_remote_copy(
            src_ref=wsend.at[0], dst_ref=wall.at[source],
            send_sem=wsend_sem.at[source], recv_sem=wrecv_sem.at[source],
            device_id={"tmpl": lax.rem(source, bands), "tm": lax.div(source, bands)},
            device_id_type=MESH,
        )

    def arrive(k, carry):
        window_arrival(k).wait_recv()
        return carry

    lax.fori_loop(1, group, arrive, 0)
    everything = wall[...].reshape(nsft, LANES)

    step = 128

    for r in range(my_rows * grid // step):
        at = slice(r * step, (r + 1) * step)
        total = jnp.dot(mask[at, :], everything, preferred_element_type=F32)
        hi = total.astype(BF16)
        lo = (total - hi.astype(F32)).astype(BF16)
        both = jnp.concatenate([hi, lo], axis=1)
        ra, ia, rb, ib = [jnp.dot(both, base, preferred_element_type=F32) for base in bases]
        wa, wb, wc = sums[at, 0:1], sums[at, 1:2], sums[at, 2:3]
        inverse = 1.0 / (wa * wb - wc * wc)
        top = wb * (ra * ra + ia * ia) + wa * (rb * rb + ib * ib) - (2.0 * wc) * (ra * rb + ia * ib)
        stat = top * inverse
        fstat_ref[at, :] = stat
        best = stat[:, 0:LANES]
        for q in range(1, width // LANES):
            best = jnp.maximum(best, stat[:, q * LANES:(q + 1) * LANES])
        lsend[0:1, at] = jnp.max(jnp.transpose(best), axis=0, keepdims=True)

    def loud_copy(k):
        peer = lax.rem(t_me + k, bands)
        return pltpu.make_async_remote_copy(
            src_ref=lsend, dst_ref=lrecv.at[t_me],
            send_sem=lsend_sem.at[peer], recv_sem=lrecv_sem.at[t_me],
            device_id={"tmpl": peer}, device_id_type=MESH,
        )

    def loud_arrival(k):
        source = lax.rem(t_me + k, bands)
        return pltpu.make_async_remote_copy(
            src_ref=lsend, dst_ref=lrecv.at[source],
            send_sem=lsend_sem.at[source], recv_sem=lrecv_sem.at[source],
            device_id={"tmpl": source}, device_id_type=MESH,
        )

    def start_loud(k, carry):
        loud_copy(k).start()
        return carry

    lax.fori_loop(1, bands, start_loud, 0)

    def window_done(k, carry):
        peer = lax.rem(me + k, group)
        window_copy(lax.rem(peer, bands), lax.div(peer, bands)).wait_send()
        return carry

    lax.fori_loop(1, group, window_done, 0)

    def off_done(k, carry):
        off_copy(k).wait_send()
        return carry

    lax.fori_loop(1, bands, off_done, 0)
    lrecv[t_me] = lsend[...]

    def loud_arrive(k, carry):
        loud_arrival(k).wait_recv()
        return carry

    lax.fori_loop(1, bands, loud_arrive, 0)
    most = lrecv[0]
    for t in range(1, bands):
        most = jnp.maximum(most, lrecv[t])
    for j in range(my_rows):
        loud_ref[j:j + 1, :] = most[:, j * grid:(j + 1) * grid]

    def loud_done(k, carry):
        loud_copy(k).wait_send()
        return carry

    lax.fori_loop(1, bands, loud_done, 0)


def body(spectra, offsets, fractions, antenna, starts, durations):
    bands = lax.axis_size("tmpl")
    times = lax.axis_size("tm")
    rows, _, bins = spectra.shape
    nb = offsets.shape[1]
    width = fractions.shape[0]
    nsft = antenna.shape[0]
    grid = starts.shape[0]
    my_rows = grid // times
    chunks = bins // bands // LANES
    group = bands * times
    cells = my_rows * grid
    cfg = (bands, times, rows, nb, chunks, nsft, grid, my_rows)
    vmem = pl.BlockSpec(memory_space=pltpu.VMEM)
    anywhere = pl.BlockSpec(memory_space=pltpu.HBM)
    fstat, loudest = pl.pallas_call(
        functools.partial(fused, cfg),
        out_shape=(
            jax.ShapeDtypeStruct((cells, width), F32),
            jax.ShapeDtypeStruct((my_rows, grid), F32),
        ),
        in_specs=[anywhere] * 6,
        out_specs=(vmem, vmem),
        scratch_shapes=[
            pltpu.VMEM((nb, offsets.shape[0]), jnp.int32),
            pltpu.VMEM((1, width), F32),
            pltpu.VMEM((4, nsft), F32),
            pltpu.SMEM((grid,), jnp.int32),
            pltpu.SMEM((grid,), jnp.int32),
            pltpu.SemaphoreType.DMA((5,)),
            pltpu.VMEM((rows, 4, bins), BF16),
            pltpu.VMEM((bins // LANES, rows * 4, LANES), F32),
            pltpu.VMEM((bands, nb, LANES), jnp.int32),
            pltpu.VMEM((bands, nb, LANES), jnp.int32),
            pltpu.VMEM((bands * nb, rows, LANES), jnp.int32),
            pltpu.VMEM((bands, rows, LANES), BF16),
            pltpu.VMEM((group, rows, LANES), BF16),
            pltpu.VMEM((cells, nsft), BF16),
            pltpu.VMEM((1, cells), F32),
            pltpu.VMEM((bands, 1, cells), F32),
            pltpu.SemaphoreType.DMA,
            pltpu.SemaphoreType.DMA((bands,)),
            pltpu.SemaphoreType.DMA((bands,)),
            pltpu.SemaphoreType.DMA((group,)),
            pltpu.SemaphoreType.DMA((group,)),
            pltpu.SemaphoreType.DMA((bands,)),
            pltpu.SemaphoreType.DMA((bands,)),
        ],
        compiler_params=pltpu.CompilerParams(
            collective_id=0, has_side_effects=True, vmem_limit_bytes=32 * 1024 * 1024
        ),
        name="transient_fstat",
    )(*[
        pltpu.with_memory_space_constraint(x, pltpu.HBM)
        for x in (offsets.T, spectra, fractions.reshape(1, width), antenna.T, starts, durations)
    ])
    return fstat.reshape(my_rows, grid, width), loudest


def solution(mesh):
    in_specs = (
        P(("grp", "tm", "tmpl"), None, None),
        P(("grp", "tm"), "tmpl"),
        P(("grp", "tmpl")),
        P("grp", None),
        P("grp"),
        P("grp"),
    )
    out_specs = (P("tm", None, ("grp", "tmpl")), P(("grp", "tm"), None))
    return jax.shard_map(body, mesh=mesh, in_specs=in_specs, out_specs=out_specs, check_vma=False)
```

```python
import functools

import jax
import jax.numpy as jnp
from jax import lax
from jax.experimental import pallas as pl
from jax.experimental.pallas import tpu as pltpu
from jax.sharding import PartitionSpec as P

W = 16
LANES = 128
F32 = jnp.float32
BF16 = jnp.bfloat16
MESH = pl.DeviceIdType.MESH


def split3(x):
    hi = x.astype(BF16)
    rest = x - hi.astype(F32)
    mid = rest.astype(BF16)
    return hi, mid, (rest - mid.astype(F32)).astype(BF16)


def fused(
    cfg,
    off_in, spec_ref, frac_in, ant_in, starts_in, dur_in,
    fstat_ref, loud_ref,
    off_ref, frac_ref, ant_ref, starts_ref, dur_ref, small_sem,
    xbuf, xf, off_send, off_recv, places, wsend, wall, mask, lsend, lrecv,
    spec_sem, osend_sem, orecv_sem, wsend_sem, wrecv_sem, lsend_sem, lrecv_sem,
):
    bands, times, rows, nb, chunks, nsft, grid, my_rows = cfg
    t_me = lax.axis_index("tmpl")
    m_me = lax.axis_index("tm")
    group = bands * times
    me = m_me * bands + t_me

    spec_copy = pltpu.make_async_copy(spec_ref, xbuf, spec_sem)
    small = [
        pltpu.make_async_copy(source, target, small_sem.at[n])
        for n, (source, target) in enumerate(
            [(off_in, off_ref), (starts_in, starts_ref), (dur_in, dur_ref), (ant_in, ant_ref), (frac_in, frac_ref)]
        )
    ]
    for copy in small:
        copy.start()
    spec_copy.start()

    barrier = pltpu.get_barrier_semaphore()

    def greet(k, carry):
        peer = lax.rem(me + k, group)
        pl.semaphore_signal(
            barrier, inc=1,
            device_id={"tmpl": lax.rem(peer, bands), "tm": lax.div(peer, bands)},
            device_id_type=MESH,
        )
        return carry

    lax.fori_loop(1, group, greet, 0)

    small[0].wait()
    off_send[...] = jnp.zeros_like(off_send)
    for t in range(bands):
        off_send[t, :, 0:rows] = off_ref[:, t * rows:(t + 1) * rows]
    off_recv[t_me] = off_send[t_me]
    small[1].wait()
    small[2].wait()
    row = lax.broadcasted_iota(jnp.int32, (grid, LANES), 0)
    begin = jnp.zeros((grid, LANES), jnp.int32)
    for i in range(grid):
        begin = jnp.where(row == i, starts_ref[i], begin)
    begin = jnp.concatenate([begin] * (nsft // LANES), axis=1)
    sft = lax.broadcasted_iota(jnp.int32, (grid, nsft), 1)
    since = sft - begin
    for j in range(my_rows):
        length = dur_ref[m_me * my_rows + j]
        inside = jnp.logical_and(since >= 0, since < length)
        mask[j * grid:(j + 1) * grid, :] = inside.astype(F32).astype(BF16)
    small[3].wait()
    small[4].wait()
    pl.semaphore_wait(barrier, group - 1)

    def off_copy(k):
        peer = lax.rem(t_me + k, bands)
        return pltpu.make_async_remote_copy(
            src_ref=off_send.at[peer], dst_ref=off_recv.at[t_me],
            send_sem=osend_sem.at[peer], recv_sem=orecv_sem.at[t_me],
            device_id={"tmpl": peer}, device_id_type=MESH,
        )

    def off_arrival(k):
        source = lax.rem(t_me + k, bands)
        return pltpu.make_async_remote_copy(
            src_ref=off_send.at[source], dst_ref=off_recv.at[source],
            send_sem=osend_sem.at[source], recv_sem=orecv_sem.at[source],
            device_id={"tmpl": source}, device_id_type=MESH,
        )

    def start_off(k, carry):
        off_copy(k).start()
        return carry

    lax.fori_loop(1, bands, start_off, 0)

    spec_copy.wait()

    def widen(i, carry):
        pair = jnp.concatenate(
            [xbuf[2 * i].astype(F32), xbuf[2 * i + 1].astype(F32)], axis=0
        )
        at = pl.ds(pl.multiple_of(i * 8, 8), 8)
        for ch in range(bands * chunks):
            xf[ch, at, :] = pair[:, ch * LANES:(ch + 1) * LANES]
        return carry

    lax.fori_loop(0, rows // 2, widen, 0)

    lane = lax.broadcasted_iota(jnp.int32, (rows, LANES), 1)
    lane_m = lane % W
    lane_b = (lane // W) % nb
    lane_c = lane // (W * nb)
    ant_t = jnp.transpose(
        jnp.concatenate([ant_ref[...], jnp.zeros((4, nsft), F32)], axis=0)
    )
    mine = jnp.zeros((rows, 8), F32)
    for slot in range(group):
        mine = jnp.where(slot == me, ant_t[slot * rows:(slot + 1) * rows, :], mine)
    upper = lane_c < 2
    coef_p = jnp.where(upper, mine[:, 0:1], mine[:, 2:3])
    coef_q = jnp.where(upper, mine[:, 1:2], mine[:, 3:4])
    even = (lane_c % 2) == 0

    def window_copy(t, m):
        return pltpu.make_async_remote_copy(
            src_ref=wsend.at[t], dst_ref=wall.at[me],
            send_sem=wsend_sem.at[m * bands + t], recv_sem=wrecv_sem.at[me],
            device_id={"tmpl": t, "tm": m}, device_id_type=MESH,
        )

    def off_arrive(k, carry):
        off_arrival(k).wait_recv()
        return carry

    lax.fori_loop(1, bands, off_arrive, 0)
    columns = jnp.transpose(
        jnp.concatenate([off_recv[t] for t in range(bands)], axis=0)
    )[0:rows, :]
    for t in range(bands):
        for b in range(nb):
            at = t * nb + b
            places[at] = jnp.broadcast_to(columns[:, at:at + 1], (rows, LANES))

    def pick(k, carry):
        t = lax.rem(t_me + k, bands)

        picked = [None] * 4
        for b in range(nb):
            begin_b = places[t * nb + b]
            wanted = begin_b // LANES + (lane < begin_b % LANES).astype(jnp.int32)
            spot = (begin_b + lane_m) % LANES
            source = [jnp.zeros((rows, LANES), F32) for _ in range(4)]
            for ch in range(chunks):
                here = wanted == ch
                for c in range(4):
                    piece = xf[t * chunks + ch, pl.ds(c, rows, stride=4), :]
                    source[c] = jnp.where(here, piece, source[c])
            for c in range(4):
                got = jnp.take_along_axis(source[c], spot, axis=1, mode="promise_in_bounds")
                picked[c] = got if b == 0 else jnp.where(lane_b == b, got, picked[c])
        one = jnp.where(even, picked[0], picked[1])
        two = jnp.where(even, picked[2], picked[3])
        wsend[t] = (coef_p * one + coef_q * two).astype(BF16)
        for m in range(times):
            @pl.when(jnp.logical_or(t != t_me, m != m_me))
            def _():
                window_copy(t, m).start()
        return carry

    lax.fori_loop(1, bands + 1, pick, 0, unroll=2)
    wall[me] = wsend[t_me]

    ant = ant_ref[...]
    a1, a2, b1, b2 = ant[0:1], ant[1:2], ant[2:3], ant[3:4]
    terms = jnp.concatenate(
        [a1 * a1 + a2 * a2, b1 * b1 + b2 * b2, a1 * b1 + a2 * b2, jnp.zeros((5, nsft), F32)],
        axis=0,
    )
    nt = (((1,), (1,)), ((), ()))
    sums = 0.0
    for piece in split3(terms):
        sums = sums + lax.dot_general(mask[...], piece, nt, preferred_element_type=F32)

    width = frac_ref.shape[1]
    fracs = frac_ref[...]
    shift = lax.broadcasted_iota(jnp.int32, (W, width), 0)
    alternate = (1 - 2 * (shift % 2)).astype(F32)
    distance = fracs + (W // 2 - 1) - shift.astype(F32)
    dirichlet = alternate * jnp.sin(jnp.pi * fracs) / (jnp.pi * distance)
    tiled = jnp.concatenate([dirichlet] * (4 * nb), axis=0)
    feature = lax.broadcasted_iota(jnp.int32, tiled.shape, 0)
    block = lax.broadcasted_iota(jnp.int32, tiled.shape, 1) // (width // nb)
    same = (feature // W) % nb == block
    bases = []
    for c in range(4):
        base = jnp.where(jnp.logical_and(same, feature // (W * nb) == c), tiled, 0.0)
        base = base.astype(BF16)
        bases.append(jnp.concatenate([base, base], axis=0))

    def window_arrival(k):
        source = lax.rem(me + k, group)
        return pltpu.make_async_remote_copy(
            src_ref=wsend.at[0], dst_ref=wall.at[source],
            send_sem=wsend_sem.at[source], recv_sem=wrecv_sem.at[source],
            device_id={"tmpl": lax.rem(source, bands), "tm": lax.div(source, bands)},
            device_id_type=MESH,
        )

    def arrive(k, carry):
        window_arrival(k).wait_recv()
        return carry

    lax.fori_loop(1, group, arrive, 0)
    everything = wall[...].reshape(nsft, LANES)

    step = 256

    for r in range(my_rows * grid // step):
        at = slice(r * step, (r + 1) * step)
        total = jnp.dot(mask[at, :], everything, preferred_element_type=F32)
        hi = total.astype(BF16)
        lo = (total - hi.astype(F32)).astype(BF16)
        both = jnp.concatenate([hi, lo], axis=1)
        ra, ia, rb, ib = [jnp.dot(both, base, preferred_element_type=F32) for base in bases]
        wa, wb, wc = sums[at, 0:1], sums[at, 1:2], sums[at, 2:3]
        inverse = 1.0 / (wa * wb - wc * wc)
        top = wb * (ra * ra + ia * ia) + wa * (rb * rb + ib * ib) - (2.0 * wc) * (ra * rb + ia * ib)
        stat = top * inverse
        fstat_ref[at, :] = stat
        best = stat[:, 0:LANES]
        for q in range(1, width // LANES):
            best = jnp.maximum(best, stat[:, q * LANES:(q + 1) * LANES])
        lsend[0:1, at] = jnp.max(jnp.transpose(best), axis=0, keepdims=True)

    def loud_copy(k):
        peer = lax.rem(t_me + k, bands)
        return pltpu.make_async_remote_copy(
            src_ref=lsend, dst_ref=lrecv.at[t_me],
            send_sem=lsend_sem.at[peer], recv_sem=lrecv_sem.at[t_me],
            device_id={"tmpl": peer}, device_id_type=MESH,
        )

    def loud_arrival(k):
        source = lax.rem(t_me + k, bands)
        return pltpu.make_async_remote_copy(
            src_ref=lsend, dst_ref=lrecv.at[source],
            send_sem=lsend_sem.at[source], recv_sem=lrecv_sem.at[source],
            device_id={"tmpl": source}, device_id_type=MESH,
        )

    def start_loud(k, carry):
        loud_copy(k).start()
        return carry

    lax.fori_loop(1, bands, start_loud, 0)

    def window_done(k, carry):
        peer = lax.rem(me + k, group)
        window_copy(lax.rem(peer, bands), lax.div(peer, bands)).wait_send()
        return carry

    lax.fori_loop(1, group, window_done, 0)

    def off_done(k, carry):
        off_copy(k).wait_send()
        return carry

    lax.fori_loop(1, bands, off_done, 0)
    lrecv[t_me] = lsend[...]

    def loud_arrive(k, carry):
        loud_arrival(k).wait_recv()
        return carry

    lax.fori_loop(1, bands, loud_arrive, 0)
    most = lrecv[0]
    for t in range(1, bands):
        most = jnp.maximum(most, lrecv[t])
    for j in range(my_rows):
        loud_ref[j:j + 1, :] = most[:, j * grid:(j + 1) * grid]

    def loud_done(k, carry):
        loud_copy(k).wait_send()
        return carry

    lax.fori_loop(1, bands, loud_done, 0)


def body(spectra, offsets, fractions, antenna, starts, durations):
    bands = lax.axis_size("tmpl")
    times = lax.axis_size("tm")
    rows, _, bins = spectra.shape
    nb = offsets.shape[1]
    width = fractions.shape[0]
    nsft = antenna.shape[0]
    grid = starts.shape[0]
    my_rows = grid // times
    chunks = bins // bands // LANES
    group = bands * times
    cells = my_rows * grid
    cfg = (bands, times, rows, nb, chunks, nsft, grid, my_rows)
    vmem = pl.BlockSpec(memory_space=pltpu.VMEM)
    anywhere = pl.BlockSpec(memory_space=pltpu.HBM)
    fstat, loudest = pl.pallas_call(
        functools.partial(fused, cfg),
        out_shape=(
            jax.ShapeDtypeStruct((cells, width), F32),
            jax.ShapeDtypeStruct((my_rows, grid), F32),
        ),
        in_specs=[anywhere] * 6,
        out_specs=(vmem, vmem),
        scratch_shapes=[
            pltpu.VMEM((nb, offsets.shape[0]), jnp.int32),
            pltpu.VMEM((1, width), F32),
            pltpu.VMEM((4, nsft), F32),
            pltpu.SMEM((grid,), jnp.int32),
            pltpu.SMEM((grid,), jnp.int32),
            pltpu.SemaphoreType.DMA((5,)),
            pltpu.VMEM((rows, 4, bins), BF16),
            pltpu.VMEM((bins // LANES, rows * 4, LANES), F32),
            pltpu.VMEM((bands, nb, LANES), jnp.int32),
            pltpu.VMEM((bands, nb, LANES), jnp.int32),
            pltpu.VMEM((bands * nb, rows, LANES), jnp.int32),
            pltpu.VMEM((bands, rows, LANES), BF16),
            pltpu.VMEM((group, rows, LANES), BF16),
            pltpu.VMEM((cells, nsft), BF16),
            pltpu.VMEM((1, cells), F32),
            pltpu.VMEM((bands, 1, cells), F32),
            pltpu.SemaphoreType.DMA,
            pltpu.SemaphoreType.DMA((bands,)),
            pltpu.SemaphoreType.DMA((bands,)),
            pltpu.SemaphoreType.DMA((group,)),
            pltpu.SemaphoreType.DMA((group,)),
            pltpu.SemaphoreType.DMA((bands,)),
            pltpu.SemaphoreType.DMA((bands,)),
        ],
        compiler_params=pltpu.CompilerParams(
            collective_id=0, has_side_effects=True, vmem_limit_bytes=32 * 1024 * 1024
        ),
        name="transient_fstat",
    )(*[
        pltpu.with_memory_space_constraint(x, pltpu.HBM)
        for x in (offsets.T, spectra, fractions.reshape(1, width), antenna.T, starts, durations)
    ])
    return fstat.reshape(my_rows, grid, width), loudest


def solution(mesh):
    in_specs = (
        P(("grp", "tm", "tmpl"), None, None),
        P(("grp", "tm"), "tmpl"),
        P(("grp", "tmpl")),
        P("grp", None),
        P("grp"),
        P("grp"),
    )
    out_specs = (P("tm", None, ("grp", "tmpl")), P(("grp", "tm"), None))
    return jax.shard_map(body, mesh=mesh, in_specs=in_specs, out_specs=out_specs, check_vma=False)
```
